32 devices in a mesh: cells: 4 (over y, x), levels: 8 (over z, core).
Axes of the slice: x: 2, y: 2, z: 4, core: 2. Of those that a mesh axis runs over, the one named last changes fastest.
Arguments:
- populations: float32 [2048, 4096], P('cells', 'levels'), may hold values from 0.05 to 2
- face_speed: float32 [2049], replicated, may hold values from -1 to 1
- cell_class: int32 [2048, 1], P('cells'), may hold values from 0 to 3; in each aligned block of 512 rows (0 to 511, 512 to 1023, ...) at most 256 rows name the same one
- class_offset: bfloat16 [2048], P('cells'), may hold values from -1 to 1
- rate_matrix: bfloat16 [4, 4096, 4096], P('cells', 'levels'), may hold values from -0.09375 to 0.09375
- slope_matrix: bfloat16 [4, 4096, 4096], P('cells', 'levels'), may hold values from -0.09375 to 0.09375
- rate_scale: float32 [4, 4096], P('cells', 'levels'), may hold values from 0.2 to 2
- slope_scale: float32 [4, 4096], P('cells', 'levels'), may hold values from 0.2 to 2
Outputs:
- sources: float32 [2048, 4096], P('cells', 'levels')
- updated: float32 [2048, 4096], P('cells', 'levels')
The draws below stay inside these ranges and needn't reach their ends.
Inputs may be any that keep to these rules, and one draw needn't show every extreme that they name: `cell_class`: among the cells of one index of the cells axis (aligned blocks of 512 cells) no class is named by more than 256 cells.
All inputs are finite; a program needn't handle non-finite values.
Results may differ from the reference program's by a relative error of at most 0.0029.
Values may be sent and summed in bfloat16 or wider, within the bound.
No kernel may reach another device: no remote copies, remote signals or barrier semaphores. Data moves between devices by JAX's collectives and lax.ppermute only.
A program may use at most 64 MiB of HBM per device.

```python
import math
import jax
import jax.numpy as jnp
import numpy as np
from jax import lax

CELL_DEV = 512
L = 4096
CELLS = 2048
CLASSES = 4
CAP = 256
N_CELLS = 4


def level_of(own_key, shape, split, least, top_value):
    def one(axis_at, blocks):
        heights = jax.random.uniform(jax.random.fold_in(jax.random.fold_in(own_key, 6), axis_at), (blocks,), jnp.float32, least / len(split), top_value / len(split))
        return jnp.repeat(jnp.exp(heights), shape[axis_at] // blocks).reshape((-1,) + (1,) * (len(shape) - axis_at - 1))

    level = one(*split[0])
    for cut in split[1:]:
        level = level * one(*cut)
    return level


def routed_block(stream_key, own, number, rows, count, top, bound, lean):
    sequence = jax.random.permutation(stream_key, count)
    packed, usual = portions_of(count, rows * top, bound, lean, True), portions_of(count, rows * top, bound, lean, False)
    places = jnp.arange(count)

    def named(tallies, rotation):
        used = int((tallies > 0).sum())
        fixed = max(1, used // 4)
        shifted = fixed + (places - fixed + rotation * (used - fixed)) % max(1, count - fixed)
        return jnp.zeros((count,), jnp.int32).at[sequence[jnp.where(places < fixed, places, shifted)]].set(jnp.asarray(tallies, jnp.int32))

    tallies = jnp.where(number % 4 == 0, named(packed, number // 4), named(usual, number - number // 4 - 1))
    mixed = jax.random.permutation(jax.random.fold_in(own, 3), count)
    donor, taker = mixed[0:count // 2 * 2:2], mixed[1:count // 2 * 2:2]
    margin = jnp.minimum(tallies[donor] - 1, bound - tallies[taker]) // 2
    margin = jnp.where((donor == sequence[0]) | (taker == sequence[0]) | (tallies[taker] == 0), 0, jnp.maximum(margin, 0))
    shifted = jax.random.randint(jax.random.fold_in(own, 4), (count // 2,), 0, 1 << 20) % (margin + 1)
    tallies = tallies.at[donor].add(-shifted).at[taker].add(shifted)
    members = jnp.searchsorted(jnp.cumsum(tallies), jnp.arange(rows * top), side="right").astype(jnp.int32)
    table = members.reshape(top, rows).T
    table = table[jax.random.permutation(jax.random.fold_in(own, 1), rows)]
    rotation = jax.random.randint(jax.random.fold_in(own, 2), (rows, 1), 0, top)
    return jnp.take_along_axis(table, (jnp.arange(top)[None, :] + rotation) % top, axis=1)


def portions_of(number_of, total, limit, skew, full):
    weights = [(1 << 20) // math.isqrt(standing ** skew) + 1 for standing in range(1, number_of + 1)]
    largest = limit if full else min(limit, max(-(-total // number_of), total * weights[0] // sum(weights)))
    least = 1 if total - largest >= number_of - 1 else 0
    holding, rest = [largest] + [least] * (number_of - 1), total - largest - least * (number_of - 1)
    while rest > 0:
        candidates = [i for i in range(1, number_of) if holding[i] < largest] or [i for i in range(1, number_of) if holding[i] < limit]
        whole, left = sum([weights[i] for i in candidates]), rest
        for i in candidates:
            addition = min(limit - holding[i], max(1, left * weights[i] // whole), rest)
            holding[i] = holding[i] + addition
            rest = rest - addition
    return np.array(holding)


def bell_draw(stream_key, extent, width, limit, split=(), kind=jnp.bfloat16):
    array = width * jax.random.normal(stream_key, extent, jnp.float32)
    if split:
        array = array * level_of(stream_key, extent, split, -0.22, 0.18)
    return jnp.clip(array, -limit, limit).astype(kind)


def setup_inputs(seed: int = 0) -> dict:
    keys = jax.random.split(jax.random.key(seed), 9)
    populations = jnp.clip(jnp.exp(math.log(2.0) - 3.6888794 * jax.random.uniform(keys[0], (CELLS, L), jnp.float32) ** level_of(keys[0], (CELLS, L), ((0, 4), (1, 8)), -0.2, 0.2)), 0.05, 2.0)
    face_speed = jnp.clip(jax.random.uniform(keys[1], (CELLS + 1,), jnp.float32, -1.0, 1.0), -1.0, 1.0)
    cell_class_keys = jax.random.split(jax.random.fold_in(keys[2], 1), CELLS // CELL_DEV)
    cell_class_turns = jax.random.permutation(jax.random.fold_in(keys[2], 3), CELLS // CELL_DEV)
    cell_class = jax.vmap(lambda own, number: routed_block(jax.random.fold_in(keys[2], 2), own, number, CELL_DEV, CLASSES, 1, CAP, 2))(cell_class_keys, cell_class_turns).reshape((CELLS, 1))
    class_offset = jnp.clip(jax.random.uniform(keys[3], (CELLS,), jnp.float32, -1.0, 1.0) * level_of(keys[3], (CELLS,), ((0, 4),), -0.4, 0.0), -1.0, 1.0).astype(jnp.bfloat16)
    rate_matrix = bell_draw(keys[4], (CLASSES, L, L), L ** -0.5, 0.09375, ((0, 4), (1, 8)))
    slope_matrix = bell_draw(keys[5], (CLASSES, L, L), L ** -0.5, 0.09375, ((0, 4), (1, 8)))
    rate_scale = jnp.clip(jnp.exp(math.log(2.0) - 2.3025851 * jax.random.uniform(keys[6], (CLASSES, L), jnp.float32) ** level_of(keys[6], (CLASSES, L), ((0, 4), (1, 8)), -0.2, 0.2)), 0.2, 2.0)
    slope_scale = jnp.clip(jnp.exp(math.log(2.0) - 2.3025851 * jax.random.uniform(keys[7], (CLASSES, L), jnp.float32) ** level_of(keys[7], (CLASSES, L), ((0, 4), (1, 8)), -0.2, 0.2)), 0.2, 2.0)
    return dict(populations=populations, face_speed=face_speed, cell_class=cell_class, class_offset=class_offset, rate_matrix=rate_matrix, slope_matrix=slope_matrix, rate_scale=rate_scale, slope_scale=slope_scale)


cfl_number = 0.4
step_size = 0.5
spread = 1.25


def transport(populations, face_speed):
    padded = jnp.pad(populations, ((1, 1), (0, 0)))
    left = padded[:-1]
    right = padded[1:]
    face_flux = 0.5 * face_speed[:, None] * (left + right) - 0.5 * spread * (right - left)
    return populations + cfl_number * (face_flux[:-1] - face_flux[1:])


def reference(populations, face_speed, cell_class, class_offset, rate_matrix, slope_matrix, rate_scale, slope_scale):
    transported = transport(populations, face_speed)
    narrow = transported.astype(jnp.bfloat16)
    classes = cell_class[:, 0]
    bucket = N_CELLS * CAP

    def one_class(totals, class_id):
        picked = jnp.argsort((classes != class_id).astype(jnp.int32), stable=True)[:bucket].astype(jnp.int32)
        in_class = classes[picked] == class_id
        rows = narrow[picked]
        rate_part = jnp.dot(rows, rate_matrix[class_id].T, preferred_element_type=jnp.float32)
        slope_part = jnp.dot(rows, slope_matrix[class_id].T, preferred_element_type=jnp.float32)
        offsets = class_offset[picked].astype(jnp.float32)[:, None]
        values = rate_scale[class_id][None, :] * rate_part + slope_scale[class_id][None, :] * offsets * slope_part
        values = jnp.where(in_class[:, None], values, jnp.zeros_like(values))
        return totals.at[picked].add(values), None

    start = jnp.zeros(transported.shape, jnp.float32)
    sources, _ = lax.scan(one_class, start, jnp.arange(CLASSES, dtype=jnp.int32))
    updated = transported + step_size * sources
    return sources, updated
```

```python
import jax
import jax.numpy as jnp
from jax import lax
from jax.sharding import PartitionSpec as P

cfl_number = 0.4
step_size = 0.5
spread = 1.25
CORES = 2


def contract(rows, matrix):
    return lax.dot_general(
        rows, matrix, (((1,), (1,)), ((), ())), preferred_element_type=jnp.float32
    )


def partner(i, j, n):
    return i ^ j if n & (n - 1) == 0 else (j - i) % n


def line_order(n):
    table = []
    for z in range(n):
        arrivals = []
        for s in range(1, n):
            if z - s >= 0:
                arrivals.append((s, 1))
            if z + s < n:
                arrivals.append((s, -1))
        table.append(arrivals)
    return table


def gather_line(x, place, n, cores):
    table = line_order(n)
    got = {}
    for step in (1, -1):
        held = x
        for s in range(1, n):
            pairs = []
            for z in range(n):
                if 0 <= z - s * step < n:
                    pairs += [((z - step) * cores + c, z * cores + c) for c in range(cores)]
            held = lax.ppermute(held, "levels", pairs)
            got[(s, step)] = held
    chunks = [(x, place)]
    for i in range(n - 1):
        keys = [table[z][i] for z in range(n)]
        block = got[keys[0]]
        source = place - keys[0][0] * keys[0][1]
        for key in dict.fromkeys(keys):
            if key == keys[0]:
                continue
            here = jnp.zeros((), jnp.bool_)
            for z in range(n):
                if keys[z] == key:
                    here = here | (place == z)
            block = jnp.where(here, got[key], block)
            source = jnp.where(here, place - key[0] * key[1], source)
        chunks.append((block, source))
    return chunks


def shards(
    populations,
    face_speed,
    cell_class,
    class_offset,
    rate_matrix,
    slope_matrix,
    rate_scale,
    slope_scale,
):
    row_count, width = populations.shape
    owners = lax.axis_size("cells")
    cell = lax.axis_index("cells")
    level_count = lax.axis_size("levels")
    level = lax.axis_index("levels")
    cores = CORES if level_count % CORES == 0 else 1
    line = level_count // cores
    place, core = level // cores, level % cores
    capacity = 2 * row_count // owners

    up = [(i, i + 1) for i in range(owners - 1)]
    down = [(j, i) for i, j in up]
    before = lax.ppermute(populations[-1:], "cells", up)
    after = lax.ppermute(populations[:1], "cells", down)
    speeds = lax.dynamic_slice_in_dim(face_speed, cell * row_count, row_count + 1)
    padded = jnp.concatenate([before, populations, after], axis=0)
    left = padded[:-1]
    right = padded[1:]
    face_flux = 0.5 * speeds[:, None] * (left + right) - 0.5 * spread * (right - left)
    transported = populations + cfl_number * (face_flux[:-1] - face_flux[1:])
    narrow = transported.astype(jnp.bfloat16)

    classes = cell_class[:, 0]
    if owners & (owners - 1) == 0:
        window = classes ^ cell
    else:
        window = (classes + cell) % owners
    one_hot = window[None, :] == jnp.arange(owners, dtype=jnp.int32)[:, None]
    earlier = (
        jnp.arange(row_count)[:, None] < jnp.arange(row_count)[None, :]
    ).astype(jnp.bfloat16)
    ranks = lax.dot_general(
        one_hot.astype(jnp.bfloat16), earlier, (((1,), (0,)), ((), ())),
        preferred_element_type=jnp.float32,
    )
    rank = jnp.sum(jnp.where(one_hot, ranks, 0.0), axis=0).astype(jnp.int32)
    slot = window * capacity + rank
    place_rows = (
        jnp.arange(owners * capacity, dtype=jnp.int32)[:, None] == slot[None, :]
    ).astype(jnp.bfloat16)

    def spread_rows(block):
        return lax.dot_general(
            place_rows, block, (((1,), (0,)), ((), ())), preferred_element_type=jnp.float32
        ).astype(jnp.bfloat16).reshape(owners, capacity, -1)

    def exchange(blocks):
        out = []
        for j in range(owners):
            pairs = [(i, partner(i, j, owners)) for i in range(owners)]
            if all(a == b for a, b in pairs):
                out.append(blocks[j])
            else:
                out.append(lax.ppermute(blocks[j], "cells", pairs))
        return out

    offset_rows = spread_rows(jnp.broadcast_to(class_offset[:, None], (row_count, 128)))
    offsets = jnp.concatenate(exchange(offset_rows), axis=0)[:, :1].astype(jnp.float32)

    swap = [(z * cores + c, z * cores + (cores - 1 - c)) for z in range(line) for c in range(cores)]
    rate_rows = rate_matrix[0]
    slope_rows = slope_matrix[0]
    rate_part = jnp.zeros((owners * capacity, rate_rows.shape[0]), jnp.float32)
    slope_part = rate_part
    for block, source in gather_line(narrow, place, line, cores):
        routed = jnp.concatenate(exchange(spread_rows(block)), axis=0)
        pieces = [(routed, source * cores + core)]
        if cores > 1:
            other = lax.ppermute(routed, "levels", swap)
            pieces.append((other, source * cores + (cores - 1 - core)))
        for piece, at in pieces:
            rate_part += contract(
                piece, lax.dynamic_slice_in_dim(rate_rows, at * width, width, axis=1)
            )
            slope_part += contract(
                piece, lax.dynamic_slice_in_dim(slope_rows, at * width, width, axis=1)
            )
    rate_gain = rate_scale[0][None, :]
    slope_gain = slope_scale[0][None, :]
    values = (rate_gain * rate_part + slope_gain * offsets * slope_part).astype(jnp.bfloat16)
    returned = jnp.concatenate(exchange(values.reshape(owners, capacity, -1)), axis=0)
    sources = lax.dot_general(
        place_rows, returned, (((0,), (0,)), ((), ())), preferred_element_type=jnp.float32
    )
    updated = transported + step_size * sources
    return (sources, updated)


def solution(mesh):
    in_specs = (
        P("cells", "levels"),
        P(),
        P("cells", None),
        P("cells"),
        P("cells", "levels", None),
        P("cells", "levels", None),
        P("cells", "levels"),
        P("cells", "levels"),
    )
    out_specs = (P("cells", "levels"), P("cells", "levels"))
    return jax.shard_map(shards, mesh=mesh, in_specs=in_specs, out_specs=out_specs, check_vma=False)
```
